512 devices in a mesh: depth: 8 (over x, core), strip: 64 (over y, z).
Axes of the slice: x: 4, y: 4, z: 16, core: 2. Of those that a mesh axis runs over, the one named last changes fastest.
Arguments:
- surface: float32 [2, 4, 1024, 1024], P(None, None, 'strip'), may hold values from -6 to 6
- velocity_class: int32 [8, 1024, 1024], P('depth', 'strip'), may hold values from 0 to 7
- table: float32 [2, 8, 2, 10], replicated, may hold values from -2 to 2
Outputs:
- image: float32 [8, 1024, 1024], P('depth', 'strip')
The draws below stay inside these ranges and needn't reach their ends.
All inputs are finite; a program needn't handle non-finite values.
Results may differ from the reference program's by a relative error of at most 0.00017.
Values sent between devices are 32-bit elements; how exact they have to be, the bound alone decides.
No kernel may reach another device: no remote copies, remote signals or barrier semaphores. Data moves between devices by JAX's collectives and lax.ppermute only.
A program may use at most 64 MiB of HBM per device.

```python
import math
import jax
import jax.numpy as jnp

NY = 1024
FREQS = 2
PASSES = 9
CLASSES = 8
TERMS = 10
NX = 1024
DEPTHS = 8


def draw_table(key, part):
    theta_key = jax.random.fold_in(key, 11)
    radius_key = jax.random.fold_in(key, 12)
    theta = jnp.exp(jax.random.uniform(theta_key, (FREQS, CLASSES), jnp.float32, math.log(2.0), math.log(6.0)))
    radius = jax.random.uniform(radius_key, (FREQS, CLASSES), jnp.float32, 0.85, 1.0)
    node_angle = (jnp.arange(64, dtype=jnp.float32) + 0.5) * (math.pi / 64.0)
    phase = theta[:, :, None] * jnp.cos(node_angle)[None, None, :]
    real_value = radius[:, :, None] * jnp.cos(phase)
    imag_value = radius[:, :, None] * jnp.sin(phase)
    degrees = jnp.arange(TERMS, dtype=jnp.float32)
    basis = jnp.cos(degrees[:, None] * node_angle[None, :]) * jnp.where(degrees == 0, 1.0, 2.0)[:, None] / 64.0
    real_coef = jnp.einsum('fcm,km->fck', real_value, basis)
    imag_coef = jnp.einsum('fcm,km->fck', imag_value, basis)
    return jnp.stack([real_coef, imag_coef], axis=2).astype(jnp.float32)


def touch_ends(entries, key, low, top_value):
    longest = entries.shape.index(max(entries.shape))
    spots = []
    for shift in (0, 1):
        where = [jax.random.randint(jax.random.fold_in(key, axis), (), 0, length) for axis, length in enumerate(entries.shape)]
        where[longest] = (where[longest] + shift) % entries.shape[longest]
        spots.append(tuple(where))
    return entries.at[spots[0]].set(low).at[spots[1]].set(top_value)


def steps_of(key, dims, pieces, least, largest):
    factor_of, own = 1.0, jax.random.fold_in(key, 6)
    for dim, blocks in pieces:
        draws = jnp.exp(jax.random.uniform(jax.random.fold_in(own, dim), (blocks,), jnp.float32, least / len(pieces), largest / len(pieces)))
        factor_of = factor_of * jnp.repeat(draws, dims[dim] // blocks).reshape([-1 if axis == dim else 1 for axis in range(len(dims))])
    return factor_of


def scatter_about(rng, dims, scale, limit, cuts=(), kind=jnp.bfloat16):
    loudness = steps_of(rng, dims, cuts, -0.22, 0.18) if cuts else 1.0
    entries = jax.random.normal(rng, dims, jnp.float32) * scale * loudness
    return jnp.minimum(jnp.maximum(entries, -limit), limit).astype(kind)


def setup_inputs(seed: int = 0) -> dict:
    streams_of = jax.random.split(jax.random.key(seed), 4)
    surface = scatter_about(streams_of[0], (FREQS, 4, NX, NY), 1.0, 6.0, ((2, 64),), jnp.float32)
    velocity_class = touch_ends(jax.random.randint(streams_of[1], (DEPTHS, NX, NY), 0, CLASSES), jax.random.fold_in(streams_of[1], 1), 0, CLASSES - 1).astype(jnp.int32)
    table = draw_table(jax.random.fold_in(streams_of[3], 71), 0)
    return dict(surface=surface, velocity_class=velocity_class, table=table)


def mcclellan(field):
    lead = [(0, 0)] * (field.ndim - 2)
    padded = jnp.pad(field, lead + [(1, 1), (1, 1)])
    beside = padded[..., 2:, 1:-1] + padded[..., :-2, 1:-1] + padded[..., 1:-1, 2:] + padded[..., 1:-1, :-2]
    corners = padded[..., 2:, 2:] + padded[..., 2:, :-2] + padded[..., :-2, 2:] + padded[..., :-2, :-2]
    return -0.5 * field + 0.25 * beside + 0.125 * corners


def weigh(result, field, real_part, imag_part):
    return jnp.stack([
        result[:, 0] + (real_part * field[:, 0] - imag_part * field[:, 1]),
        result[:, 1] + (real_part * field[:, 1] + imag_part * field[:, 0]),
        result[:, 2] + (real_part * field[:, 2] + imag_part * field[:, 3]),
        result[:, 3] + (real_part * field[:, 3] - imag_part * field[:, 2])], axis=1)


def correlate(fields):
    total = jnp.zeros(fields.shape[2:], jnp.float32)
    for freq_index in range(fields.shape[0]):
        total = total + (fields[freq_index, 0] * fields[freq_index, 2] + fields[freq_index, 1] * fields[freq_index, 3])
    return total


def reference(surface, velocity_class, table):
    fields = surface
    images = []
    for level_index in range(velocity_class.shape[0]):
        classes_here = velocity_class[level_index]
        pairs = [table[:, :, :, degree][:, classes_here] for degree in range(PASSES + 1)]
        result = weigh(jnp.zeros_like(fields), fields, pairs[0][..., 0], pairs[0][..., 1])
        previous, current = fields, fields
        for degree in range(PASSES):
            if degree == 0:
                following = mcclellan(current)
            else:
                following = 2.0 * mcclellan(current) - previous
            previous, current = current, following
            result = weigh(result, current, pairs[degree + 1][..., 0], pairs[degree + 1][..., 1])
        fields = result
        images.append(correlate(fields))
    return jnp.stack(images)
```

```python
import functools

import jax
import jax.numpy as jnp
from jax import lax
from jax.experimental import pallas as pl
from jax.experimental.pallas import tpu as pltpu
from jax.sharding import PartitionSpec as P

PASSES = 9
CLASSES = 8
FIELDS = 8
LANES = 128
FUSED = 3
LAG = 2
UNROLL = 8
PHASES = (2, 3, 3)
TILE_ROWS = 32
TILE_COLS = 64
WIDE = 256
ORIGIN = (WIDE - TILE_COLS) // 2
PAD = 2


def lane_ids():
    return lax.broadcasted_iota(jnp.int32, (FIELDS, LANES), 1)


def inside(first_col, col_limit):
    cols = lane_ids() + first_col
    return jnp.where((cols >= 0) & (cols < col_limit), 0.25, 0.0).astype(jnp.float32)


def blurred(parts, lane):
    ahead = [pltpu.roll(x, LANES - 1, 1) for x in parts]
    if len(parts) == 2:
        ahead = [jnp.where(lane == LANES - 1, ahead[1], ahead[0]), ahead[1]]
    pair = [x + y for x, y in zip(parts, ahead)]
    behind = [pltpu.roll(x, 1, 1) for x in pair]
    if len(parts) == 2:
        behind = [behind[0], jnp.where(lane == 0, behind[0], behind[1])]
    return [x + y for x, y in zip(pair, behind)]


def swapped(x, sub):
    up = pltpu.roll(x, FIELDS - 1, 0)
    down = pltpu.roll(x, 1, 0)
    return jnp.where(sub % 2 == 0, up, down)


def sweep(first_degree, low, high, tiles, refs, tabs, scale):
    cur, summed, acc, crs, idx = refs
    lane = lane_ids()
    sub = lax.broadcasted_iota(jnp.int32, (FIELDS, LANES), 0)
    opening = first_degree == 0
    closing = first_degree + FUSED == PASSES
    span = range(tiles)

    def row(ref, at):
        return [ref[at, :, t * LANES : (t + 1) * LANES] for t in span]

    def put(ref, at, parts):
        for t in span:
            ref[at, :, t * LANES : (t + 1) * LANES] = parts[t]

    def step(base, offset, live, valid=None):
        at = base + offset
        live[("t", 0, offset + 1)] = row(cur, at + 1)
        for level in range(FUSED, 0, -1) if LAG > 1 else range(1, FUSED + 1):
            own = offset - (level - 1) * LAG
            if valid is not None and own < valid + level:
                if level == 1 or own >= valid + level - 1:
                    pass
                continue
            here = live[("t", level - 1, own)]
            after = live[("t", level - 1, own + 1)]
            pair = [x + y for x, y in zip(here, after)]
            both = [x + y for x, y in zip(live[("u", level - 1, own - 1)], pair)]
            live[("u", level - 1, own)] = pair
            both = blurred(both, lane)
            if opening and level == 1:
                total = [(0.5 * s) * x for s, x in zip(scale, both)]
            else:
                before = row(summed, at) if level == 1 else live[("e", level - 1, own)]
                total = [s * x - e for s, x, e in zip(scale, both, before)]
            live[("e", level, own)] = total
            live[("t", level, own)] = [e - x for e, x in zip(total, here)]
        done = offset - (FUSED - 1) * LAG
        if valid is not None and done < valid + FUSED:
            return
        place = base + done
        picks = row(idx, place)
        levels = list(range(0 if opening else 1, FUSED + 1))
        terms = [row(cur, place) if level == 0 else live[("t", level, done)] for level in levels]
        new_acc = [None] * tiles if opening else row(acc, place)
        new_crs = [None] * tiles if opening else row(crs, place)
        for level, term in zip(levels, terms):
            real_tab, imag_tab = tabs(first_degree + level)
            for t in span:
                real = jnp.take_along_axis(real_tab, picks[t], axis=1) * term[t]
                imag = jnp.take_along_axis(imag_tab, picks[t], axis=1) * term[t]
                new_acc[t] = real if new_acc[t] is None else new_acc[t] + real
                new_crs[t] = imag if new_crs[t] is None else new_crs[t] + imag
        if closing:
            put(cur, place, [x + swapped(y, sub) for x, y in zip(new_acc, new_crs)])
        else:
            put(acc, place, new_acc)
            put(crs, place, new_crs)
            put(cur, place, live[("t", FUSED, done)])
            put(summed, place, live[("e", FUSED, done)])

    def seed(live, valid, offset):
        for level in range(1, FUSED):
            edge = valid + level
            one, two = ("t", level, edge), ("t", level, edge + 1)
            if one in live and two in live and ("u", level, edge) not in live:
                live[("u", level, edge)] = [x + y for x, y in zip(live[one], live[two])]

    def keys(offset):
        out = [("t", 0, offset), ("u", 0, offset - 1)]
        for level in range(1, FUSED):
            newest = offset - 1 - (level - 1) * LAG
            for r in range(offset - (FUSED - 1) * LAG, newest + 1):
                out.append(("t", level, r))
            for r in range(offset - level * LAG, newest + 1):
                out.append(("e", level, r))
            out.append(("u", level, offset - level * LAG - 1))
        return out

    start = FUSED + (FUSED - 1) * LAG
    live = {("t", 0, 0): row(cur, low), ("t", 0, 1): row(cur, low + 1)}
    live[("u", 0, 0)] = [x + y for x, y in zip(live[("t", 0, 0)], live[("t", 0, 1)])]
    for offset in range(1, start):
        step(low, offset, live, valid=0)
        seed(live, 0, offset)
    count = high - low - 2 * FUSED
    carry = [live[key] for key in keys(start)]

    def block(base, carry, length):
        live = dict(zip(keys(0), carry))
        for offset in range(length):
            step(base, offset, live)
        return [live[key] for key in keys(length)]

    def body(i, carry):
        return block(low + start + i * UNROLL, carry, UNROLL)

    whole = count // UNROLL
    carry = lax.fori_loop(0, whole, body, carry)
    if count % UNROLL:
        block(low + start + whole * UNROLL, carry, count % UNROLL)


def centred(parts, lane):
    if len(parts) == 1:
        return parts[0]
    left, right = (pltpu.roll(x, LANES // 2, 1) for x in parts)
    return jnp.where(lane < LANES // 2, left, right)


def run_phase(steps, first_depth, tiles, flags, cur, refs, classes, tab_ref, image_ref, scale):
    halo = steps * PASSES
    lane = lane_ids()
    sub = lax.broadcasted_iota(jnp.int32, (FIELDS, LANES), 0)
    summed, acc, crs, idx = refs
    total = TILE_ROWS + 2 * halo

    @pl.when(flags[0] == 1)
    def _():
        cur[halo - 1] = jnp.zeros_like(cur[0])
        for i in range(1, halo):
            cur[halo - 1 - i] = -cur[halo - 1 + i]

    @pl.when(flags[1] == 1)
    def _():
        end = halo + TILE_ROWS
        cur[end] = jnp.zeros_like(cur[0])
        for i in range(1, halo):
            cur[end + i] = -cur[end - i]

    def tabs(degree):
        return tab_ref[degree, 0], tab_ref[degree, 1]

    for local in range(steps):
        reach = (steps - 1 - local) * PASSES
        above, own, below = classes(first_depth + local)
        depth = first_depth + local

        def spread(to, one):
            idx[to] = jnp.broadcast_to(one, idx.shape[1:]).astype(jnp.int32)

        if reach:
            for i in range(reach):
                spread(halo - reach + i, above(i, reach))
                spread(halo + TILE_ROWS + i, below(i, reach))
        for i in range(TILE_ROWS):
            spread(halo + i, own(i))
        if reach:
            @pl.when(flags[0] == 1)
            def _():
                for i in range(1, reach):
                    idx[halo - 1 - i] = idx[halo - 1 + i]

            @pl.when(flags[1] == 1)
            def _():
                end = halo + TILE_ROWS
                for i in range(1, reach):
                    idx[end + i] = idx[end - i]

        low, high = local * PASSES, total - local * PASSES
        for part in range(PASSES // FUSED):
            sweep(
                part * FUSED,
                low + part * FUSED,
                high - part * FUSED,
                tiles,
                (cur, summed, acc, crs, idx),
                tabs,
                scale,
            )

        def pictured(i, _):
            parts = [cur[halo + i, :, t * LANES : (t + 1) * LANES] for t in range(tiles)]
            field = centred(parts, lane)
            product = field * pltpu.roll(field, FIELDS - 2, 0)
            product = jnp.where(sub % 4 < 2, product, 0.0)
            image_ref[local, pl.ds(i, 1), :] = jnp.sum(product, axis=0, keepdims=True)
            return 0

        lax.fori_loop(0, TILE_ROWS, pictured, 0, unroll=4)


def class_slots():
    slots = []
    depth = 0
    for steps in PHASES:
        for local in range(steps):
            for first in range(0, (steps - 1 - local) * PASSES, PASSES):
                slots.append((depth, first))
            depth += 1
    return slots


def slot_of(depth, first):
    return class_slots().index((depth, first))


def scatter_kernel(part_ref, surface_ref, velocity_ref, out_ref, wide_ref):
    del part_ref
    columns = surface_ref.shape[-1]
    count = out_ref.shape[0]
    strip_rows = surface_ref.shape[-2]
    wide_ref[...] = jnp.zeros_like(wide_ref)
    wide_ref[0:strip_rows, LANES : LANES + columns] = surface_ref[0]
    wide_ref[strip_rows:, LANES : LANES + columns] = velocity_ref[0].astype(jnp.float32)
    for c in range(count):
        begin = LANES - ORIGIN + TILE_COLS * c
        out_ref[c] = wide_ref[:, begin : begin + WIDE]


def gather_kernel(in_ref, tile_ref, class_ref, up_ref, down_ref):
    strip_rows = in_ref.shape[1] // 2
    halo = PHASES[0] * PASSES
    for parity in range(2):
        for i in range(strip_rows):
            to = parity * strip_rows + i
            for d in range(FIELDS):
                tile_ref[to, d : d + 1, :] = in_ref[2 * d + parity, i : i + 1, :]
                class_ref[to, d : d + 1, :] = in_ref[
                    2 * d + parity, strip_rows + i : strip_rows + i + 1, :
                ]
    up_ref[0:halo] = tile_ref[0:halo]
    down_ref[0:halo] = tile_ref[TILE_ROWS - halo : TILE_ROWS]
    up_ref[halo:] = jnp.zeros_like(up_ref[halo:])
    down_ref[halo:] = jnp.zeros_like(down_ref[halo:])
    for slot, (depth, first) in enumerate(class_slots()):
        for i in range(PASSES):
            up_ref[halo + i, slot : slot + 1, :] = class_ref[first + i, depth : depth + 1, :]
            far = TILE_ROWS - PASSES - first + i
            down_ref[halo + i, slot : slot + 1, :] = class_ref[far, depth : depth + 1, :]


def class_rows(above_ref, own_ref, below_ref, base, lanes):
    def reader(depth):
        def above(i, reach):
            back = reach - 1 - i
            first = back // PASSES * PASSES
            slot = slot_of(depth, first)
            at = base + PASSES - 1 - (back - first)
            return above_ref[at, slot : slot + 1, lanes]

        def own(i):
            return own_ref[i, depth : depth + 1, lanes]

        def below(i, reach):
            first = i // PASSES * PASSES
            slot = slot_of(depth, first)
            return below_ref[base + i - first, slot : slot + 1, lanes]

        return above, own, below

    return reader


def phase_kernel(
    phase, col_limit, classes_narrow, scalars_ref, above_ref, tile_ref, below_ref, cls_above_ref,
    cls_ref, cls_below_ref, tab_ref, *rest
):
    steps = PHASES[phase]
    halo = steps * PASSES
    tiles = tile_ref.shape[-1] // LANES
    last = phase == len(PHASES) - 1
    if last:
        image_ref, cur, *refs = rest
    else:
        image_ref, out_ref, up_ref, down_ref, cur, *refs = rest
    cur[0:halo] = above_ref[0:halo]
    cur[halo : halo + TILE_ROWS] = tile_ref[...]
    cur[halo + TILE_ROWS : TILE_ROWS + 2 * halo] = below_ref[0:halo]
    first_col = scalars_ref[2] - (ORIGIN if tiles == 2 else ORIGIN - LANES // 2)
    scale = [inside(first_col + t * LANES, col_limit) for t in range(tiles)]
    reader = class_rows(
        cls_above_ref, cls_ref, cls_below_ref, PHASES[0] * PASSES if not classes_narrow else 0,
        slice(0, tiles * LANES),
    )
    run_phase(
        steps, sum(PHASES[:phase]), tiles, (scalars_ref[0], scalars_ref[1]), cur, refs, reader,
        tab_ref, image_ref, scale,
    )
    if last:
        return
    lane = lane_ids()
    out_tiles = out_ref.shape[-1] // LANES
    next_halo = PHASES[phase + 1] * PASSES

    def emit(i, _):
        parts = [cur[halo + i, :, t * LANES : (t + 1) * LANES] for t in range(tiles)]
        if out_tiles < tiles:
            parts = [centred(parts, lane)]
        for t in range(out_tiles):
            out_ref[i, :, t * LANES : (t + 1) * LANES] = parts[t]
        return 0

    lax.fori_loop(0, TILE_ROWS, emit, 0, unroll=4)
    up_ref[...] = out_ref[0:next_halo]
    down_ref[...] = out_ref[TILE_ROWS - next_halo : TILE_ROWS]


def narrow_kernel(above_ref, own_ref, below_ref, out_above, out_own, out_below):
    lane = lane_ids()
    base = PHASES[0] * PASSES
    for source, target, offset in (
        (above_ref, out_above, base), (own_ref, out_own, 0), (below_ref, out_below, base)
    ):
        for i in range(target.shape[0]):
            parts = [source[offset + i, :, t * LANES : (t + 1) * LANES] for t in range(2)]
            target[i] = centred(parts, lane)


def collect_kernel(in_ref, out_ref):
    lane = lax.broadcasted_iota(jnp.int32, (in_ref.shape[1], LANES), 1)
    shift = (LANES - TILE_COLS) // 2
    for t in range(out_ref.shape[-1] // LANES):
        left = pltpu.roll(in_ref[2 * t], LANES - shift, 1)
        right = pltpu.roll(in_ref[2 * t + 1], shift, 1)
        out_ref[0, :, t * LANES : (t + 1) * LANES] = jnp.where(lane < TILE_COLS, left, right)


def coefficient_tables(table):
    by_field = jnp.repeat(jnp.transpose(table, (3, 2, 0, 1)), 4, axis=2)
    signs = jnp.array([1.0, -1.0, -1.0, 1.0] * 2, jnp.float32)
    parts = jnp.stack([jnp.ones_like(signs), signs])
    by_field = by_field * parts[None, :, :, None]
    return jnp.pad(by_field, ((0, 0), (0, 0), (0, 0), (0, LANES - CLASSES)))


VMEM = pl.BlockSpec(memory_space=pltpu.VMEM)
SMEM = pl.BlockSpec(memory_space=pltpu.SMEM)


def shaped(*dims):
    return jax.ShapeDtypeStruct(dims, jnp.float32)


def call(kernel, out_shape, in_specs, scratch=(), name=None):
    outs = jax.tree.map(lambda _: VMEM, out_shape)
    return pl.pallas_call(
        kernel, out_shape=out_shape, in_specs=in_specs, out_specs=outs, scratch_shapes=scratch, name=name
    )


def body(surface, velocity_class, table):
    parts, strips = lax.axis_size("depth"), lax.axis_size("strip")
    part, strip = lax.axis_index("depth"), lax.axis_index("strip")
    strip_rows, columns = velocity_class.shape[1:]
    chunks = 2 * parts
    groups = [
        [p * strips + 2 * j + b for p in range(parts) for b in range(2)] for j in range(strips // 2)
    ]
    both_axes = ("depth", "strip")
    scalars = jnp.stack(
        [
            (strip < 2).astype(jnp.int32),
            (strip >= strips - 2).astype(jnp.int32),
            (2 * part + strip % 2).astype(jnp.int32) * TILE_COLS,
        ]
    )
    planes = surface.reshape((FIELDS, strip_rows, columns))
    outgoing = pl.pallas_call(
        scatter_kernel,
        out_shape=shaped(chunks, 2 * strip_rows, WIDE),
        grid_spec=pltpu.PrefetchScalarGridSpec(
            num_scalar_prefetch=1,
            grid=(1,),
            in_specs=[
                pl.BlockSpec((1, strip_rows, columns), lambda i, at: (at[0], 0, 0)),
                pl.BlockSpec((1, strip_rows, columns), lambda i, at: (0, 0, 0)),
            ],
            out_specs=pl.BlockSpec((chunks, 2 * strip_rows, WIDE), lambda i, at: (0, 0, 0)),
            scratch_shapes=[pltpu.VMEM((2 * strip_rows, columns + 3 * LANES), jnp.float32)],
        ),
        name="scatter",
    )(part.reshape((1,)), planes, velocity_class)
    incoming = lax.all_to_all(outgoing, both_axes, 0, 0, axis_index_groups=groups, tiled=True)
    tables = coefficient_tables(table)

    halos = [steps * PASSES for steps in PHASES]
    tile, classes, up, down = call(
        gather_kernel,
        (
            shaped(TILE_ROWS, FIELDS, WIDE),
            shaped(TILE_ROWS, FIELDS, WIDE),
            shaped(halos[0] + PASSES, FIELDS, WIDE),
            shaped(halos[0] + PASSES, FIELDS, WIDE),
        ),
        [VMEM],
        name="gather",
    )(incoming)
    ahead = [(s, s + 2) for s in range(strips - 2)]
    back = [(s + 2, s) for s in range(strips - 2)]

    images = []
    class_args = None
    for phase, steps in enumerate(PHASES):
        above = lax.ppermute(down, "strip", ahead)
        below = lax.ppermute(up, "strip", back)
        last = phase == len(PHASES) - 1
        width = LANES if last else WIDE
        if phase == 0:
            class_args = (above, classes, below)
            narrow_args = call(
                narrow_kernel,
                (
                    shaped(PASSES, FIELDS, LANES),
                    shaped(TILE_ROWS, FIELDS, LANES),
                    shaped(PASSES, FIELDS, LANES),
                ),
                [VMEM] * 3,
                name="narrow",
            )(*class_args)
        rows = TILE_ROWS + 2 * halos[phase]
        out_shape = [shaped(steps, TILE_ROWS, LANES)]
        if not last:
            next_width = LANES if phase + 1 == len(PHASES) - 1 else WIDE
            out_shape.append(shaped(TILE_ROWS, FIELDS, next_width))
            out_shape += [shaped(halos[phase + 1], FIELDS, next_width)] * 2
        scratch = [pltpu.VMEM((rows + PAD, FIELDS, width), jnp.float32)] * 4
        scratch.append(pltpu.VMEM((rows + PAD, FIELDS, width), jnp.int32))
        out = call(
            functools.partial(phase_kernel, phase, columns, last),
            tuple(out_shape),
            [SMEM] + [VMEM] * 7,
            scratch,
            name=f"phase{phase}",
        )(scalars, above, tile, below, *(narrow_args if last else class_args), tables)
        images.append(out[0])
        if not last:
            tile, up, down = out[1:]
    image = jnp.concatenate(images, axis=0)
    image = image.reshape((chunks, strip_rows, LANES))
    image = lax.all_to_all(image, both_axes, 0, 0, axis_index_groups=groups, tiled=True)
    return call(collect_kernel, shaped(1, strip_rows, columns), [VMEM], name="collect")(image)


def solution(mesh):
    in_specs = (P(None, None, "strip", None), P("depth", "strip", None), P())
    out_specs = P("depth", "strip", None)
    return jax.shard_map(body, mesh=mesh, in_specs=in_specs, out_specs=out_specs, check_vma=False)
```

```python
import functools

import jax
import jax.numpy as jnp
from jax import lax
from jax.experimental import pallas as pl
from jax.experimental.pallas import tpu as pltpu
from jax.sharding import PartitionSpec as P

PASSES = 9
CLASSES = 8
FIELDS = 8
LANES = 128
BLOCK = 32
PHASES = (2, 3, 3)
TILE_ROWS = 32
TILE_COLS = 64
WIDE = 256
ORIGIN = (WIDE - TILE_COLS) // 2
PAD = 8


def lane_ids():
    return lax.broadcasted_iota(jnp.int32, (FIELDS, LANES), 1)


def column_matrix(first_col, col_limit, width):
    source = lax.broadcasted_iota(jnp.int32, (width, width), 0)
    target = lax.broadcasted_iota(jnp.int32, (width, width), 1)
    apart = jnp.abs(source - target)
    weight = jnp.where(apart == 0, 0.5, jnp.where(apart == 1, 0.25, 0.0))
    cols = target + first_col
    return jnp.where((cols >= 0) & (cols < col_limit), weight, 0.0).astype(jnp.bfloat16)


def swapped(x, sub):
    up = pltpu.roll(x, FIELDS - 1, 0)
    down = pltpu.roll(x, 1, 0)
    return jnp.where(sub % 2 == 0, up, down)


def pieces(x):
    high = x.astype(jnp.bfloat16)
    rest = x - high.astype(jnp.float32)
    middle = rest.astype(jnp.bfloat16)
    low = (rest - middle.astype(jnp.float32)).astype(jnp.bfloat16)
    return jnp.concatenate([high, middle, low], axis=0)


def one_pass(degree, low, high, terms, matrix_ref):
    count = high - low
    blocks = -(-count // BLOCK)
    size = 2 * -(-count // (2 * blocks))
    width = terms.shape[-1]

    def block(i, _):
        base = low + i * size
        x = terms[degree, pl.ds(base - 1, size + 2)]
        pair = x[:-1] + x[1:]
        both = (pair[:-1] + pair[1:]).reshape((size * FIELDS, width))
        parts = jnp.dot(pieces(both), matrix_ref[...], preferred_element_type=jnp.float32)
        rows = size * FIELDS
        blurred = (parts[:rows] + parts[rows : 2 * rows]) + parts[2 * rows :]
        blurred = blurred.reshape((size, FIELDS, width))
        here = x[1:-1]
        if degree == 0:
            following = 0.5 * blurred - here
        else:
            following = (blurred - (here + here)) - terms[degree - 1, pl.ds(base, size)]
        terms[degree + 1, pl.ds(base, size)] = following
        return 0

    lax.fori_loop(0, blocks, block, 0)


def weigh(low, high, tiles, terms, coef, idx, tab_ref):
    sub = lax.broadcasted_iota(jnp.int32, (FIELDS, LANES), 0)
    signs = jnp.where((sub % 4 == 0) | (sub % 4 == 3), 1.0, -1.0)

    def pick(i, _):
        for t in range(tiles):
            here = slice(t * LANES, (t + 1) * LANES)
            picks = idx[low + i, :, here]
            for g in range(tab_ref.shape[0]):
                found = jnp.take_along_axis(tab_ref[g], picks, axis=1, mode="promise_in_bounds")
                coef[low + i, g * FIELDS : (g + 1) * FIELDS, here] = found
        return 0

    lax.fori_loop(0, high - low, pick, 0, unroll=2)

    def combine(i, _):
        at = low + i
        for t in range(tiles):
            here = slice(t * LANES, (t + 1) * LANES)

            def one(degree, part):
                first = 4 * degree + 2 * part
                a = jnp.broadcast_to(coef[at, first : first + 1, here], (FIELDS, LANES))
                b = jnp.broadcast_to(coef[at, first + 1 : first + 2, here], (FIELDS, LANES))
                return jnp.where(sub < FIELDS // 2, a, b)

            own, other = None, None
            for degree in range(PASSES + 1):
                term = terms[degree, at, :, here]
                real, imag = one(degree, 0) * term, one(degree, 1) * term
                own = real if own is None else own + real
                other = imag if other is None else other + imag
            terms[0, at, :, here] = own + swapped(signs * other, sub)
        return 0

    lax.fori_loop(0, high - low, combine, 0, unroll=2)


def centred(parts, lane):
    if len(parts) == 1:
        return parts[0]
    left, right = (pltpu.roll(x, LANES // 2, 1) for x in parts)
    return jnp.where(lane < LANES // 2, left, right)


def run_phase(steps, first_depth, tiles, flags, terms, refs, classes, tab_ref, image_ref):
    halo = steps * PASSES
    lane = lane_ids()
    sub = lax.broadcasted_iota(jnp.int32, (FIELDS, LANES), 0)
    matrix_ref, coef, idx = refs
    cur = terms.at[0]
    total = TILE_ROWS + 2 * halo

    @pl.when(flags[0] == 1)
    def _():
        cur[halo - 1] = jnp.zeros_like(cur[0])
        for i in range(1, halo):
            cur[halo - 1 - i] = -cur[halo - 1 + i]

    @pl.when(flags[1] == 1)
    def _():
        end = halo + TILE_ROWS
        cur[end] = jnp.zeros_like(cur[0])
        for i in range(1, halo):
            cur[end + i] = -cur[end - i]

    for local in range(steps):
        reach = (steps - 1 - local) * PASSES
        above, own, below = classes(first_depth + local)
        depth = first_depth + local

        def spread(to, one):
            idx[to] = jnp.broadcast_to(one, idx.shape[1:]).astype(jnp.int32)

        if reach:
            for i in range(reach):
                spread(halo - reach + i, above(i, reach))
                spread(halo + TILE_ROWS + i, below(i, reach))
        for i in range(TILE_ROWS):
            spread(halo + i, own(i))
        if reach:
            @pl.when(flags[0] == 1)
            def _():
                for i in range(1, reach):
                    idx[halo - 1 - i] = idx[halo - 1 + i]

            @pl.when(flags[1] == 1)
            def _():
                end = halo + TILE_ROWS
                for i in range(1, reach):
                    idx[end + i] = idx[end - i]

        low, high = local * PASSES, total - local * PASSES
        for degree in range(PASSES):
            one_pass(degree, low + degree + 1, high - degree - 1, terms, matrix_ref)
        weigh(low + PASSES, high - PASSES, tiles, terms, coef, idx, tab_ref)

        def pictured(i, _):
            parts = [cur[halo + i, :, t * LANES : (t + 1) * LANES] for t in range(tiles)]
            field = centred(parts, lane)
            product = field * pltpu.roll(field, FIELDS - 2, 0)
            product = jnp.where(sub % 4 < 2, product, 0.0)
            image_ref[local, pl.ds(i, 1), :] = jnp.sum(product, axis=0, keepdims=True)
            return 0

        lax.fori_loop(0, TILE_ROWS, pictured, 0, unroll=4)


def class_slots():
    slots = []
    depth = 0
    for steps in PHASES:
        for local in range(steps):
            for first in range(0, (steps - 1 - local) * PASSES, PASSES):
                slots.append((depth, first))
            depth += 1
    return slots


def slot_of(depth, first):
    return class_slots().index((depth, first))


def scatter_kernel(part_ref, surface_ref, velocity_ref, out_ref, wide_ref):
    del part_ref
    columns = surface_ref.shape[-1]
    count = out_ref.shape[0]
    strip_rows = surface_ref.shape[-2]
    wide_ref[...] = jnp.zeros_like(wide_ref)
    wide_ref[0:strip_rows, LANES : LANES + columns] = surface_ref[0]
    wide_ref[strip_rows:, LANES : LANES + columns] = velocity_ref[0].astype(jnp.float32)
    for c in range(count):
        begin = LANES - ORIGIN + TILE_COLS * c
        out_ref[c] = wide_ref[:, begin : begin + WIDE]


def gather_kernel(in_ref, tile_ref, class_ref, up_ref, down_ref):
    strip_rows = in_ref.shape[1] // 2
    halo = PHASES[0] * PASSES
    for parity in range(2):
        for i in range(strip_rows):
            to = parity * strip_rows + i
            for d in range(FIELDS):
                tile_ref[to, d : d + 1, :] = in_ref[2 * d + parity, i : i + 1, :]
                class_ref[to, d : d + 1, :] = in_ref[
                    2 * d + parity, strip_rows + i : strip_rows + i + 1, :
                ]
    up_ref[0:halo] = tile_ref[0:halo]
    down_ref[0:halo] = tile_ref[TILE_ROWS - halo : TILE_ROWS]
    up_ref[halo:] = jnp.zeros_like(up_ref[halo:])
    down_ref[halo:] = jnp.zeros_like(down_ref[halo:])
    for slot, (depth, first) in enumerate(class_slots()):
        for i in range(PASSES):
            up_ref[halo + i, slot : slot + 1, :] = class_ref[first + i, depth : depth + 1, :]
            far = TILE_ROWS - PASSES - first + i
            down_ref[halo + i, slot : slot + 1, :] = class_ref[far, depth : depth + 1, :]


def class_rows(above_ref, own_ref, below_ref, base, lanes):
    def reader(depth):
        def above(i, reach):
            back = reach - 1 - i
            first = back // PASSES * PASSES
            slot = slot_of(depth, first)
            at = base + PASSES - 1 - (back - first)
            return above_ref[at, slot : slot + 1, lanes]

        def own(i):
            return own_ref[i, depth : depth + 1, lanes]

        def below(i, reach):
            first = i // PASSES * PASSES
            slot = slot_of(depth, first)
            return below_ref[base + i - first, slot : slot + 1, lanes]

        return above, own, below

    return reader


def phase_kernel(
    phase, col_limit, classes_narrow, scalars_ref, above_ref, tile_ref, below_ref, cls_above_ref,
    cls_ref, cls_below_ref, tab_ref, *rest
):
    steps = PHASES[phase]
    halo = steps * PASSES
    tiles = tile_ref.shape[-1] // LANES
    last = phase == len(PHASES) - 1
    if last:
        image_ref, terms, *refs = rest
    else:
        image_ref, out_ref, up_ref, down_ref, terms, *refs = rest
    cur = terms.at[0]
    cur[0:halo] = above_ref[0:halo]
    cur[halo : halo + TILE_ROWS] = tile_ref[...]
    cur[halo + TILE_ROWS : TILE_ROWS + 2 * halo] = below_ref[0:halo]
    first_col = scalars_ref[2] - (ORIGIN if tiles == 2 else ORIGIN - LANES // 2)
    refs[0][...] = column_matrix(first_col, col_limit, tiles * LANES)
    reader = class_rows(
        cls_above_ref, cls_ref, cls_below_ref, PHASES[0] * PASSES if not classes_narrow else 0,
        slice(0, tiles * LANES),
    )
    run_phase(
        steps, sum(PHASES[:phase]), tiles, (scalars_ref[0], scalars_ref[1]), terms, refs, reader,
        tab_ref, image_ref,
    )
    if last:
        return
    lane = lane_ids()
    out_tiles = out_ref.shape[-1] // LANES
    next_halo = PHASES[phase + 1] * PASSES

    def emit(i, _):
        parts = [cur[halo + i, :, t * LANES : (t + 1) * LANES] for t in range(tiles)]
        if out_tiles < tiles:
            parts = [centred(parts, lane)]
        for t in range(out_tiles):
            out_ref[i, :, t * LANES : (t + 1) * LANES] = parts[t]
        return 0

    lax.fori_loop(0, TILE_ROWS, emit, 0, unroll=4)
    up_ref[...] = out_ref[0:next_halo]
    down_ref[...] = out_ref[TILE_ROWS - next_halo : TILE_ROWS]


def narrow_kernel(above_ref, own_ref, below_ref, out_above, out_own, out_below):
    lane = lane_ids()
    base = PHASES[0] * PASSES
    for source, target, offset in (
        (above_ref, out_above, base), (own_ref, out_own, 0), (below_ref, out_below, base)
    ):
        for i in range(target.shape[0]):
            parts = [source[offset + i, :, t * LANES : (t + 1) * LANES] for t in range(2)]
            target[i] = centred(parts, lane)


def collect_kernel(in_ref, out_ref):
    lane = lax.broadcasted_iota(jnp.int32, (in_ref.shape[1], LANES), 1)
    shift = (LANES - TILE_COLS) // 2
    for t in range(out_ref.shape[-1] // LANES):
        left = pltpu.roll(in_ref[2 * t], LANES - shift, 1)
        right = pltpu.roll(in_ref[2 * t + 1], shift, 1)
        out_ref[0, :, t * LANES : (t + 1) * LANES] = jnp.where(lane < TILE_COLS, left, right)


def coefficient_tables(table):
    rows = jnp.transpose(table, (3, 2, 0, 1)).reshape((-1, FIELDS, CLASSES))
    return jnp.pad(rows, ((0, 0), (0, 0), (0, LANES - CLASSES)))


VMEM = pl.BlockSpec(memory_space=pltpu.VMEM)
SMEM = pl.BlockSpec(memory_space=pltpu.SMEM)


def shaped(*dims):
    return jax.ShapeDtypeStruct(dims, jnp.float32)


def call(kernel, out_shape, in_specs, scratch=(), name=None):
    outs = jax.tree.map(lambda _: VMEM, out_shape)
    return pl.pallas_call(
        kernel, out_shape=out_shape, in_specs=in_specs, out_specs=outs, scratch_shapes=scratch, name=name
    )


def phase_scratch(phase):
    rows = TILE_ROWS + 2 * PHASES[phase] * PASSES + PAD
    width = LANES if phase == len(PHASES) - 1 else WIDE
    return [
        pltpu.VMEM((PASSES + 1, rows, FIELDS, width), jnp.float32),
        pltpu.VMEM((width, width), jnp.bfloat16),
        pltpu.VMEM((rows, 4 * (PASSES + 1), width), jnp.float32),
        pltpu.VMEM((rows, FIELDS, width), jnp.int32),
    ]


def body(surface, velocity_class, table):
    parts, strips = lax.axis_size("depth"), lax.axis_size("strip")
    part, strip = lax.axis_index("depth"), lax.axis_index("strip")
    strip_rows, columns = velocity_class.shape[1:]
    chunks = 2 * parts
    groups = [
        [p * strips + 2 * j + b for p in range(parts) for b in range(2)] for j in range(strips // 2)
    ]
    both_axes = ("depth", "strip")
    scalars = jnp.stack(
        [
            (strip < 2).astype(jnp.int32),
            (strip >= strips - 2).astype(jnp.int32),
            (2 * part + strip % 2).astype(jnp.int32) * TILE_COLS,
        ]
    )
    planes = surface.reshape((FIELDS, strip_rows, columns))
    outgoing = pl.pallas_call(
        scatter_kernel,
        out_shape=shaped(chunks, 2 * strip_rows, WIDE),
        grid_spec=pltpu.PrefetchScalarGridSpec(
            num_scalar_prefetch=1,
            grid=(1,),
            in_specs=[
                pl.BlockSpec((1, strip_rows, columns), lambda i, at: (at[0], 0, 0)),
                pl.BlockSpec((1, strip_rows, columns), lambda i, at: (0, 0, 0)),
            ],
            out_specs=pl.BlockSpec((chunks, 2 * strip_rows, WIDE), lambda i, at: (0, 0, 0)),
            scratch_shapes=[pltpu.VMEM((2 * strip_rows, columns + 3 * LANES), jnp.float32)],
        ),
        name="scatter",
    )(part.reshape((1,)), planes, velocity_class)
    incoming = lax.all_to_all(outgoing, both_axes, 0, 0, axis_index_groups=groups, tiled=True)
    tables = coefficient_tables(table)

    halos = [steps * PASSES for steps in PHASES]
    tile, classes, up, down = call(
        gather_kernel,
        (
            shaped(TILE_ROWS, FIELDS, WIDE),
            shaped(TILE_ROWS, FIELDS, WIDE),
            shaped(halos[0] + PASSES, FIELDS, WIDE),
            shaped(halos[0] + PASSES, FIELDS, WIDE),
        ),
        [VMEM],
        name="gather",
    )(incoming)
    ahead = [(s, s + 2) for s in range(strips - 2)]
    back = [(s + 2, s) for s in range(strips - 2)]

    images = []
    class_args = None
    for phase, steps in enumerate(PHASES):
        above = lax.ppermute(down, "strip", ahead)
        below = lax.ppermute(up, "strip", back)
        last = phase == len(PHASES) - 1
        if phase == 0:
            class_args = (above, classes, below)
            narrow_args = call(
                narrow_kernel,
                (
                    shaped(PASSES, FIELDS, LANES),
                    shaped(TILE_ROWS, FIELDS, LANES),
                    shaped(PASSES, FIELDS, LANES),
                ),
                [VMEM] * 3,
                name="narrow",
            )(*class_args)
        out_shape = [shaped(steps, TILE_ROWS, LANES)]
        if not last:
            next_width = LANES if phase + 1 == len(PHASES) - 1 else WIDE
            out_shape.append(shaped(TILE_ROWS, FIELDS, next_width))
            out_shape += [shaped(halos[phase + 1], FIELDS, next_width)] * 2
        scratch = phase_scratch(phase)
        out = call(
            functools.partial(phase_kernel, phase, columns, last),
            tuple(out_shape),
            [SMEM] + [VMEM] * 7,
            scratch,
            name=f"phase{phase}",
        )(scalars, above, tile, below, *(narrow_args if last else class_args), tables)
        images.append(out[0])
        if not last:
            tile, up, down = out[1:]
    image = jnp.concatenate(images, axis=0)
    image = image.reshape((chunks, strip_rows, LANES))
    image = lax.all_to_all(image, both_axes, 0, 0, axis_index_groups=groups, tiled=True)
    return call(collect_kernel, shaped(1, strip_rows, columns), [VMEM], name="collect")(image)


def solution(mesh):
    in_specs = (P(None, None, "strip", None), P("depth", "strip", None), P())
    out_specs = P("depth", "strip", None)
    return jax.shard_map(body, mesh=mesh, in_specs=in_specs, out_specs=out_specs, check_vma=False)
```

```python
import functools

import jax
import jax.numpy as jnp
from jax import lax
from jax.experimental import pallas as pl
from jax.experimental.pallas import tpu as pltpu
from jax.sharding import PartitionSpec as P

PASSES = 9
CLASSES = 8
FIELDS = 8
LANES = 128
BLOCK = 32
PHASES = (2, 3, 3)
TILE_ROWS = 32
TILE_COLS = 64
WIDE = 256
ORIGIN = (WIDE - TILE_COLS) // 2
PAD = 8


def lane_ids():
    return lax.broadcasted_iota(jnp.int32, (FIELDS, LANES), 1)


def column_matrix(first_col, col_limit, width):
    source = lax.broadcasted_iota(jnp.int32, (width, width), 0)
    target = lax.broadcasted_iota(jnp.int32, (width, width), 1)
    apart = jnp.abs(source - target)
    weight = jnp.where(apart == 0, 0.5, jnp.where(apart == 1, 0.25, 0.0))
    cols = target + first_col
    return jnp.where((cols >= 0) & (cols < col_limit), weight, 0.0).astype(jnp.bfloat16)


def swapped(x, sub):
    up = pltpu.roll(x, FIELDS - 1, 0)
    down = pltpu.roll(x, 1, 0)
    return jnp.where(sub % 2 == 0, up, down)


def pieces(x):
    high = x.astype(jnp.bfloat16)
    rest = x - high.astype(jnp.float32)
    middle = rest.astype(jnp.bfloat16)
    low = (rest - middle.astype(jnp.float32)).astype(jnp.bfloat16)
    return jnp.concatenate([high, middle, low], axis=0)


def one_pass(degree, low, high, terms, matrix_ref):
    count = high - low
    blocks = -(-count // BLOCK)
    width = terms.shape[-1]
    step = 2 if width > LANES else 4
    size = step * -(-count // (step * blocks))

    def block(i, _):
        base = low + i * size
        x = terms[degree, pl.ds(base - 1, size + 2)]
        pair = x[:-1] + x[1:]
        both = (pair[:-1] + pair[1:]).reshape((size * FIELDS, width))
        parts = jnp.dot(pieces(both), matrix_ref[...], preferred_element_type=jnp.float32)
        rows = size * FIELDS
        blurred = (parts[:rows] + parts[rows : 2 * rows]) + parts[2 * rows :]
        blurred = blurred.reshape((size, FIELDS, width))
        here = x[1:-1]
        if degree == 0:
            following = 0.5 * blurred - here
        else:
            following = (blurred - (here + here)) - terms[degree - 1, pl.ds(base, size)]
        terms[degree + 1, pl.ds(base, size)] = following
        return 0

    lax.fori_loop(0, blocks, block, 0)


def weigh(low, high, tiles, terms, coef, idx, tab_ref):
    sub = lax.broadcasted_iota(jnp.int32, (FIELDS, LANES), 0)
    signs = jnp.where((sub % 4 == 0) | (sub % 4 == 3), 1.0, -1.0)

    def pick(i, _):
        for t in range(tiles):
            here = slice(t * LANES, (t + 1) * LANES)
            picks = idx[low + i, :, here]
            for g in range(tab_ref.shape[0]):
                found = jnp.take_along_axis(tab_ref[g], picks, axis=1, mode="promise_in_bounds")
                coef[low + i, g * FIELDS : (g + 1) * FIELDS, here] = found
        return 0

    lax.fori_loop(0, high - low, pick, 0, unroll=4)

    def combine(i, _):
        at = low + i
        for t in range(tiles):
            here = slice(t * LANES, (t + 1) * LANES)

            def one(degree, part):
                first = 4 * degree + 2 * part
                a = jnp.broadcast_to(coef[at, first : first + 1, here], (FIELDS, LANES))
                b = jnp.broadcast_to(coef[at, first + 1 : first + 2, here], (FIELDS, LANES))
                return jnp.where(sub < FIELDS // 2, a, b)

            own, other = None, None
            for degree in range(PASSES + 1):
                term = terms[degree, at, :, here]
                real, imag = one(degree, 0) * term, one(degree, 1) * term
                own = real if own is None else own + real
                other = imag if other is None else other + imag
            terms[0, at, :, here] = own + swapped(signs * other, sub)
        return 0

    lax.fori_loop(0, high - low, combine, 0, unroll=4)


def centred(parts, lane):
    if len(parts) == 1:
        return parts[0]
    left, right = (pltpu.roll(x, LANES // 2, 1) for x in parts)
    return jnp.where(lane < LANES // 2, left, right)


def run_phase(steps, first_depth, tiles, flags, terms, refs, classes, tab_ref, image_ref):
    halo = steps * PASSES
    lane = lane_ids()
    sub = lax.broadcasted_iota(jnp.int32, (FIELDS, LANES), 0)
    matrix_ref, coef, idx = refs
    cur = terms.at[0]
    total = TILE_ROWS + 2 * halo

    @pl.when(flags[0] == 1)
    def _():
        cur[halo - 1] = jnp.zeros_like(cur[0])
        for i in range(1, halo):
            cur[halo - 1 - i] = -cur[halo - 1 + i]

    @pl.when(flags[1] == 1)
    def _():
        end = halo + TILE_ROWS
        cur[end] = jnp.zeros_like(cur[0])
        for i in range(1, halo):
            cur[end + i] = -cur[end - i]

    for local in range(steps):
        reach = (steps - 1 - local) * PASSES
        above, own, below = classes(first_depth + local)
        depth = first_depth + local

        def spread(to, one):
            idx[to] = jnp.broadcast_to(one, idx.shape[1:]).astype(jnp.int32)

        if reach:
            for i in range(reach):
                spread(halo - reach + i, above(i, reach))
                spread(halo + TILE_ROWS + i, below(i, reach))
        for i in range(TILE_ROWS):
            spread(halo + i, own(i))
        if reach:
            @pl.when(flags[0] == 1)
            def _():
                for i in range(1, reach):
                    idx[halo - 1 - i] = idx[halo - 1 + i]

            @pl.when(flags[1] == 1)
            def _():
                end = halo + TILE_ROWS
                for i in range(1, reach):
                    idx[end + i] = idx[end - i]

        low, high = local * PASSES, total - local * PASSES
        for degree in range(PASSES):
            one_pass(degree, low + degree + 1, high - degree - 1, terms, matrix_ref)
        weigh(low + PASSES, high - PASSES, tiles, terms, coef, idx, tab_ref)

        def pictured(i, _):
            parts = [cur[halo + i, :, t * LANES : (t + 1) * LANES] for t in range(tiles)]
            field = centred(parts, lane)
            product = field * pltpu.roll(field, FIELDS - 2, 0)
            product = jnp.where(sub % 4 < 2, product, 0.0)
            image_ref[local, pl.ds(i, 1), :] = jnp.sum(product, axis=0, keepdims=True)
            return 0

        lax.fori_loop(0, TILE_ROWS, pictured, 0, unroll=4)


def class_slots():
    slots = []
    depth = 0
    for steps in PHASES:
        for local in range(steps):
            for first in range(0, (steps - 1 - local) * PASSES, PASSES):
                slots.append((depth, first))
            depth += 1
    return slots


def slot_of(depth, first):
    return class_slots().index((depth, first))


def scatter_kernel(part_ref, surface_ref, velocity_ref, out_ref, wide_ref):
    del part_ref
    columns = surface_ref.shape[-1]
    count = out_ref.shape[0]
    strip_rows = surface_ref.shape[-2]
    wide_ref[...] = jnp.zeros_like(wide_ref)
    wide_ref[0:strip_rows, LANES : LANES + columns] = surface_ref[0]
    wide_ref[strip_rows:, LANES : LANES + columns] = velocity_ref[0].astype(jnp.float32)
    for c in range(count):
        begin = LANES - ORIGIN + TILE_COLS * c
        out_ref[c] = wide_ref[:, begin : begin + WIDE]


def gather_kernel(in_ref, tile_ref, class_ref, up_ref, down_ref):
    strip_rows = in_ref.shape[1] // 2
    halo = PHASES[0] * PASSES
    for parity in range(2):
        for i in range(strip_rows):
            to = parity * strip_rows + i
            for d in range(FIELDS):
                tile_ref[to, d : d + 1, :] = in_ref[2 * d + parity, i : i + 1, :]
                class_ref[to, d : d + 1, :] = in_ref[
                    2 * d + parity, strip_rows + i : strip_rows + i + 1, :
                ]
    up_ref[0:halo] = tile_ref[0:halo]
    down_ref[0:halo] = tile_ref[TILE_ROWS - halo : TILE_ROWS]
    up_ref[halo:] = jnp.zeros_like(up_ref[halo:])
    down_ref[halo:] = jnp.zeros_like(down_ref[halo:])
    for slot, (depth, first) in enumerate(class_slots()):
        for i in range(PASSES):
            up_ref[halo + i, slot : slot + 1, :] = class_ref[first + i, depth : depth + 1, :]
            far = TILE_ROWS - PASSES - first + i
            down_ref[halo + i, slot : slot + 1, :] = class_ref[far, depth : depth + 1, :]


def class_rows(above_ref, own_ref, below_ref, base, lanes):
    def reader(depth):
        def above(i, reach):
            back = reach - 1 - i
            first = back // PASSES * PASSES
            slot = slot_of(depth, first)
            at = base + PASSES - 1 - (back - first)
            return above_ref[at, slot : slot + 1, lanes]

        def own(i):
            return own_ref[i, depth : depth + 1, lanes]

        def below(i, reach):
            first = i // PASSES * PASSES
            slot = slot_of(depth, first)
            return below_ref[base + i - first, slot : slot + 1, lanes]

        return above, own, below

    return reader


def phase_kernel(
    phase, col_limit, classes_narrow, scalars_ref, above_ref, tile_ref, below_ref, cls_above_ref,
    cls_ref, cls_below_ref, tab_ref, *rest
):
    steps = PHASES[phase]
    halo = steps * PASSES
    tiles = tile_ref.shape[-1] // LANES
    last = phase == len(PHASES) - 1
    if last:
        image_ref, terms, *refs = rest
    else:
        image_ref, out_ref, up_ref, down_ref, terms, *refs = rest
    cur = terms.at[0]
    cur[0:halo] = above_ref[0:halo]
    cur[halo : halo + TILE_ROWS] = tile_ref[...]
    cur[halo + TILE_ROWS : TILE_ROWS + 2 * halo] = below_ref[0:halo]
    first_col = scalars_ref[2] - (ORIGIN if tiles == 2 else ORIGIN - LANES // 2)
    refs[0][...] = column_matrix(first_col, col_limit, tiles * LANES)
    reader = class_rows(
        cls_above_ref, cls_ref, cls_below_ref, PHASES[0] * PASSES if not classes_narrow else 0,
        slice(0, tiles * LANES),
    )
    run_phase(
        steps, sum(PHASES[:phase]), tiles, (scalars_ref[0], scalars_ref[1]), terms, refs, reader,
        tab_ref, image_ref,
    )
    if last:
        return
    lane = lane_ids()
    out_tiles = out_ref.shape[-1] // LANES
    next_halo = PHASES[phase + 1] * PASSES

    def emit(i, _):
        parts = [cur[halo + i, :, t * LANES : (t + 1) * LANES] for t in range(tiles)]
        if out_tiles < tiles:
            parts = [centred(parts, lane)]
        for t in range(out_tiles):
            out_ref[i, :, t * LANES : (t + 1) * LANES] = parts[t]
        return 0

    lax.fori_loop(0, TILE_ROWS, emit, 0, unroll=4)
    up_ref[...] = out_ref[0:next_halo]
    down_ref[...] = out_ref[TILE_ROWS - next_halo : TILE_ROWS]


def narrow_kernel(above_ref, own_ref, below_ref, out_above, out_own, out_below):
    lane = lane_ids()
    base = PHASES[0] * PASSES
    for source, target, offset in (
        (above_ref, out_above, base), (own_ref, out_own, 0), (below_ref, out_below, base)
    ):
        for i in range(target.shape[0]):
            parts = [source[offset + i, :, t * LANES : (t + 1) * LANES] for t in range(2)]
            target[i] = centred(parts, lane)


def collect_kernel(in_ref, out_ref):
    lane = lax.broadcasted_iota(jnp.int32, (in_ref.shape[1], LANES), 1)
    shift = (LANES - TILE_COLS) // 2
    for t in range(out_ref.shape[-1] // LANES):
        left = pltpu.roll(in_ref[2 * t], LANES - shift, 1)
        right = pltpu.roll(in_ref[2 * t + 1], shift, 1)
        out_ref[0, :, t * LANES : (t + 1) * LANES] = jnp.where(lane < TILE_COLS, left, right)


def coefficient_tables(table):
    rows = jnp.transpose(table, (3, 2, 0, 1)).reshape((-1, FIELDS, CLASSES))
    return jnp.pad(rows, ((0, 0), (0, 0), (0, LANES - CLASSES)))


VMEM = pl.BlockSpec(memory_space=pltpu.VMEM)
SMEM = pl.BlockSpec(memory_space=pltpu.SMEM)


def shaped(*dims):
    return jax.ShapeDtypeStruct(dims, jnp.float32)


def call(kernel, out_shape, in_specs, scratch=(), name=None):
    outs = jax.tree.map(lambda _: VMEM, out_shape)
    return pl.pallas_call(
        kernel, out_shape=out_shape, in_specs=in_specs, out_specs=outs, scratch_shapes=scratch, name=name
    )


def phase_scratch(phase):
    rows = TILE_ROWS + 2 * PHASES[phase] * PASSES + PAD
    width = LANES if phase == len(PHASES) - 1 else WIDE
    return [
        pltpu.VMEM((PASSES + 1, rows, FIELDS, width), jnp.float32),
        pltpu.VMEM((width, width), jnp.bfloat16),
        pltpu.VMEM((rows, 4 * (PASSES + 1), width), jnp.float32),
        pltpu.VMEM((rows, FIELDS, width), jnp.int32),
    ]


def body(surface, velocity_class, table):
    parts, strips = lax.axis_size("depth"), lax.axis_size("strip")
    part, strip = lax.axis_index("depth"), lax.axis_index("strip")
    strip_rows, columns = velocity_class.shape[1:]
    chunks = 2 * parts
    groups = [
        [p * strips + 2 * j + b for p in range(parts) for b in range(2)] for j in range(strips // 2)
    ]
    both_axes = ("depth", "strip")
    scalars = jnp.stack(
        [
            (strip < 2).astype(jnp.int32),
            (strip >= strips - 2).astype(jnp.int32),
            (2 * part + strip % 2).astype(jnp.int32) * TILE_COLS,
        ]
    )
    planes = surface.reshape((FIELDS, strip_rows, columns))
    outgoing = pl.pallas_call(
        scatter_kernel,
        out_shape=shaped(chunks, 2 * strip_rows, WIDE),
        grid_spec=pltpu.PrefetchScalarGridSpec(
            num_scalar_prefetch=1,
            grid=(1,),
            in_specs=[
                pl.BlockSpec((1, strip_rows, columns), lambda i, at: (at[0], 0, 0)),
                pl.BlockSpec((1, strip_rows, columns), lambda i, at: (0, 0, 0)),
            ],
            out_specs=pl.BlockSpec((chunks, 2 * strip_rows, WIDE), lambda i, at: (0, 0, 0)),
            scratch_shapes=[pltpu.VMEM((2 * strip_rows, columns + 3 * LANES), jnp.float32)],
        ),
        name="scatter",
    )(part.reshape((1,)), planes, velocity_class)
    incoming = lax.all_to_all(outgoing, both_axes, 0, 0, axis_index_groups=groups, tiled=True)
    tables = coefficient_tables(table)

    halos = [steps * PASSES for steps in PHASES]
    tile, classes, up, down = call(
        gather_kernel,
        (
            shaped(TILE_ROWS, FIELDS, WIDE),
            shaped(TILE_ROWS, FIELDS, WIDE),
            shaped(halos[0] + PASSES, FIELDS, WIDE),
            shaped(halos[0] + PASSES, FIELDS, WIDE),
        ),
        [VMEM],
        name="gather",
    )(incoming)
    ahead = [(s, s + 2) for s in range(strips - 2)]
    back = [(s + 2, s) for s in range(strips - 2)]

    images = []
    class_args = None
    for phase, steps in enumerate(PHASES):
        above = lax.ppermute(down, "strip", ahead)
        below = lax.ppermute(up, "strip", back)
        last = phase == len(PHASES) - 1
        if phase == 0:
            class_args = (above, classes, below)
            narrow_args = call(
                narrow_kernel,
                (
                    shaped(PASSES, FIELDS, LANES),
                    shaped(TILE_ROWS, FIELDS, LANES),
                    shaped(PASSES, FIELDS, LANES),
                ),
                [VMEM] * 3,
                name="narrow",
            )(*class_args)
        out_shape = [shaped(steps, TILE_ROWS, LANES)]
        if not last:
            next_width = LANES if phase + 1 == len(PHASES) - 1 else WIDE
            out_shape.append(shaped(TILE_ROWS, FIELDS, next_width))
            out_shape += [shaped(halos[phase + 1], FIELDS, next_width)] * 2
        scratch = phase_scratch(phase)
        out = call(
            functools.partial(phase_kernel, phase, columns, last),
            tuple(out_shape),
            [SMEM] + [VMEM] * 7,
            scratch,
            name=f"phase{phase}",
        )(scalars, above, tile, below, *(narrow_args if last else class_args), tables)
        images.append(out[0])
        if not last:
            tile, up, down = out[1:]
    image = jnp.concatenate(images, axis=0)
    image = image.reshape((chunks, strip_rows, LANES))
    image = lax.all_to_all(image, both_axes, 0, 0, axis_index_groups=groups, tiled=True)
    return call(collect_kernel, shaped(1, strip_rows, columns), [VMEM], name="collect")(image)


def solution(mesh):
    in_specs = (P(None, None, "strip", None), P("depth", "strip", None), P())
    out_specs = P("depth", "strip", None)
    return jax.shard_map(body, mesh=mesh, in_specs=in_specs, out_specs=out_specs, check_vma=False)
```
